32 devices in a mesh: dp: 8 (over z, y), vocab: 4 (over x, core).
Axes of the slice: x: 2, y: 2, z: 4, core: 2. Of those that a mesh axis runs over, the one named last changes fastest.
Arguments:
- tokens: bfloat16 [1024, 7168], P('dp'), may hold values from -6 to 6
- expert_hidden: bfloat16 [1024, 8, 1024], P('dp'), may hold values from -6 to 6
- routes: int32 [1024, 8], P('dp'), may hold values from 0 to 15, all different within a row; in each aligned block of 32 rows (0 to 31, 32 to 63, ...) at most 24 rows name the same one
- route_weight: float32 [1024, 8], P('dp'), may hold values from 0.05 to 0.45
- expert_weight: bfloat16 [32, 512, 7168], P(('dp', 'vocab')), may hold values from -0.1875 to 0.1875
- norm_gain: float32 [7168], replicated, may hold values from 0.5 to 1.5
- head_weight: bfloat16 [7168, 114688], P(None, ('dp', 'vocab')), may hold values from -8 to 8
- targets: int32 [1024], P('dp'), may hold values from 0 to 114687
- rollout_logprob: float32 [1024], P('dp'), may hold values from -21 to -13
- advantages: float32 [1024], P('dp'), may hold values from -5 to 5
Outputs:
- layer_out: bfloat16 [1024, 7168], P('dp')
- token_logprob: float32 [1024], P('dp')
- token_loss: float32 [1024], P('dp')
The draws below stay inside these ranges and needn't reach their ends.
Inputs may be any that keep to these rules, and one draw needn't show every extreme that they name: The 8 routes of a token name different experts; among the routes of one aligned block of 32 token rows, no expert is named more than 24 times.
All inputs are finite; a program needn't handle non-finite values.
Results may differ from the reference program's by a relative error of at most 0.02.
Values may be sent and summed in bfloat16 or wider, within the bound.
A program may use at most 192 MiB of HBM per device.

```python
import math
import jax
import jax.numpy as jnp
import numpy as np
from jax import lax

D = 7168
HE = 1024
TOPK = 8
VOCAB = 114688
EXPERTS = 16
SUB = 32
CAP = 24
TOKENS = 1024


def draw_head_weight(key, part):
    first, second = jax.random.split(key, 2)
    columns = jnp.arange(VOCAB, dtype=jnp.float32)
    rough = jnp.exp(jax.random.uniform(first, (VOCAB,), jnp.float32, jnp.log(0.7), jnp.log(1.4)))
    scale = (1.5 + 2.5 * columns / VOCAB) * rough / jnp.sqrt(jnp.float32(D))
    values = jax.random.normal(second, (D, VOCAB), jnp.float32) * scale[None, :]
    values = jnp.clip(values, -8.0, 8.0)
    return values.astype(jnp.bfloat16)


def with_ends(drawn, stream_key, low, largest):
    longest = drawn.shape.index(max(drawn.shape))
    spots = []
    for shift in (0, 1):
        where = [jax.random.randint(jax.random.fold_in(stream_key, axis), (), 0, length) for axis, length in enumerate(drawn.shape)]
        where[longest] = (where[longest] + shift) % drawn.shape[longest]
        spots.append(tuple(where))
    return drawn.at[spots[0]].set(low).at[spots[1]].set(largest)


def shard_levels(own_key, dims, shards, low, top_value):
    def one(position, blocks):
        draws = jax.random.uniform(jax.random.fold_in(jax.random.fold_in(own_key, 6), position), (blocks,), jnp.float32, low / len(shards), top_value / len(shards))
        return jnp.repeat(jnp.exp(draws), dims[position] // blocks).reshape((-1,) + (1,) * (len(dims) - position - 1))

    loudness = one(*shards[0])
    for cut in shards[1:]:
        loudness = loudness * one(*cut)
    return loudness


def assign_block(rng, own, number, rows, amount, top, reach, lean):
    sequence = jax.random.permutation(rng, amount)
    packed, usual = load_shares(amount, rows * top, reach, lean, True), load_shares(amount, rows * top, reach, lean, False)
    places = jnp.arange(amount)

    def named(tallies, rotation):
        used = int((tallies > 0).sum())
        fixed = max(1, used // 4)
        passed = fixed + (places - fixed + rotation * (used - fixed)) % max(1, amount - fixed)
        return jnp.zeros((amount,), jnp.int32).at[sequence[jnp.where(places < fixed, places, passed)]].set(jnp.asarray(tallies, jnp.int32))

    tallies = jnp.where(number % 4 == 0, named(packed, number // 4), named(usual, number - number // 4 - 1))
    mixed = jax.random.permutation(jax.random.fold_in(own, 3), amount)
    source_of, sink = mixed[0:amount // 2 * 2:2], mixed[1:amount // 2 * 2:2]
    room = jnp.minimum(tallies[source_of] - 1, reach - tallies[sink]) // 2
    room = jnp.where((source_of == sequence[0]) | (sink == sequence[0]) | (tallies[sink] == 0), 0, jnp.maximum(room, 0))
    passed = jax.random.randint(jax.random.fold_in(own, 4), (amount // 2,), 0, 1 << 20) % (room + 1)
    tallies = tallies.at[source_of].add(-passed).at[sink].add(passed)
    items = jnp.searchsorted(jnp.cumsum(tallies), jnp.arange(rows * top), side="right").astype(jnp.int32)
    listing = items.reshape(top, rows).T
    listing = listing[jax.random.permutation(jax.random.fold_in(own, 1), rows)]
    rotation = jax.random.randint(jax.random.fold_in(own, 2), (rows, 1), 0, top)
    return jnp.take_along_axis(listing, (jnp.arange(top)[None, :] + rotation) % top, axis=1)


def load_shares(number_of, total, most, skew, full):
    portions = [(1 << 20) // math.isqrt(rank ** skew) + 1 for rank in range(1, number_of + 1)]
    largest = most if full else min(most, max(-(-total // number_of), total * portions[0] // sum(portions)))
    least = 1 if total - largest >= number_of - 1 else 0
    holding, spare = [largest] + [least] * (number_of - 1), total - largest - least * (number_of - 1)
    while spare > 0:
        movable = [i for i in range(1, number_of) if holding[i] < largest] or [i for i in range(1, number_of) if holding[i] < most]
        whole, budget = sum([portions[i] for i in movable]), spare
        for i in movable:
            more = min(most - holding[i], max(1, budget * portions[i] // whole), spare)
            holding[i] = holding[i] + more
            spare = spare - more
    return np.array(holding)


def bell_draw(key, shape, scale, limit, cuts=(), kind=jnp.bfloat16):
    result = jax.random.normal(key, shape, jnp.float32) * scale
    if len(cuts) > 0:
        result = shard_levels(key, shape, cuts, -0.22, 0.18) * result
    return jnp.clip(result, min=-limit, max=limit).astype(kind)


def setup_inputs(seed: int = 0) -> dict:
    keys = jax.random.split(jax.random.key(seed), 11)
    tokens = bell_draw(keys[0], (TOKENS, D), 1.0, 6.0, ((0, 8),))
    expert_hidden = bell_draw(keys[1], (TOKENS, TOPK, HE), 1.0, 6.0, ((0, 8),))
    routes_keys = jax.random.split(jax.random.fold_in(keys[2], 1), TOKENS // SUB)
    routes_turns = jax.random.permutation(jax.random.fold_in(keys[2], 3), TOKENS // SUB)
    routes = jax.vmap(lambda own, number: assign_block(jax.random.fold_in(keys[2], 2), own, number, SUB, EXPERTS, TOPK, CAP, 2))(routes_keys, routes_turns).reshape((TOKENS, TOPK))
    route_weight = jnp.clip(0.05 + 0.39999999 * jax.random.uniform(keys[3], (TOKENS, TOPK), jnp.float32) ** shard_levels(keys[3], (TOKENS, TOPK), ((0, 8),), -0.2, 0.2), 0.05, 0.45)
    expert_weight = bell_draw(keys[4], (2 * EXPERTS, HE // 2, D), HE ** -0.5, 0.1875, ((0, 32),))
    norm_gain = jnp.clip(1.0 + 0.1 * jax.random.normal(keys[5], (D,), jnp.float32), 0.5, 1.5)
    head_weight = draw_head_weight(jax.random.fold_in(keys[10], 71), 0)
    targets = with_ends(jax.random.randint(keys[7], (TOKENS,), 0, VOCAB), jax.random.fold_in(keys[7], 1), 0, VOCAB - 1).astype(jnp.int32)
    rollout_logprob = jnp.clip(-21.0 + 8.0 * jax.random.uniform(keys[8], (TOKENS,), jnp.float32) ** shard_levels(keys[8], (TOKENS,), ((0, 8),), -0.2, 0.2), -21.0, -13.0)
    advantages = bell_draw(keys[9], (TOKENS,), 1.0, 5.0, ((0, 8),), jnp.float32)
    return {"tokens": tokens, "expert_hidden": expert_hidden, "routes": routes, "route_weight": route_weight, "expert_weight": expert_weight, "norm_gain": norm_gain, "head_weight": head_weight, "targets": targets, "rollout_logprob": rollout_logprob, "advantages": advantages}


norm_epsilon = 1e-06
clip_low = 0.8
clip_high = 1.2
dual_bound = 3.0

def rms_scale(values, norm_gain):
    widened = values.astype(jnp.float32)
    mean_square = lax.optimization_barrier(jnp.mean(widened * widened, axis=-1, keepdims=True))
    return (widened * lax.rsqrt(mean_square + norm_epsilon) * norm_gain).astype(jnp.bfloat16)

def clipped_loss(logprob, rollout_logprob, advantages):
    ratio = jnp.exp(logprob - rollout_logprob)
    surrogate = jnp.minimum(ratio * advantages, jnp.clip(ratio, clip_low, clip_high) * advantages)
    bounded = jnp.where(advantages < 0.0, jnp.maximum(surrogate, dual_bound * advantages), surrogate)
    return -bounded

def apply_expert(operands):
    rows_in, weight = operands
    half_width = rows_in.shape[1] // 2
    lower_part = jnp.dot(rows_in[:, :half_width], weight[:half_width], preferred_element_type=jnp.float32).astype(jnp.bfloat16)
    upper_part = jnp.dot(rows_in[:, half_width:], weight[half_width:], preferred_element_type=jnp.float32).astype(jnp.bfloat16)
    return (lower_part, upper_part)

def reference(tokens, expert_hidden, routes, route_weight, expert_weight, norm_gain, head_weight, targets, rollout_logprob, advantages):
    blocks = TOKENS // SUB
    routes_blocked = routes.reshape(blocks, SUB * TOPK)
    onehot = (routes_blocked[:, :, None] == jnp.arange(EXPERTS, dtype=jnp.int32)[None, None, :]).astype(jnp.int32)
    before = jnp.cumsum(onehot, axis=1) - onehot
    slot_index = lax.optimization_barrier(jnp.sum(before * onehot, axis=2))
    buffer_row = (jnp.arange(blocks, dtype=jnp.int32)[:, None] * CAP + slot_index).reshape(-1).astype(jnp.int32)
    expert_ids = routes_blocked.reshape(-1).astype(jnp.int32)
    hidden_rows = expert_hidden.reshape(-1, HE)
    buffer = jnp.zeros((EXPERTS, blocks * CAP, HE), expert_hidden.dtype).at[expert_ids, buffer_row].set(hidden_rows)
    weights_full = expert_weight.reshape(EXPERTS, HE, D)
    lower_out, upper_out = lax.map(apply_expert, (buffer, weights_full))
    route_out = lower_out[expert_ids, buffer_row].astype(jnp.float32) + upper_out[expert_ids, buffer_row].astype(jnp.float32)
    route_out = route_out.reshape(TOKENS, TOPK, D)
    moe = lax.optimization_barrier(jnp.sum(route_out * route_weight[:, :, None], axis=1))
    layer_out = (tokens.astype(jnp.float32) + moe).astype(jnp.bfloat16)
    normed = rms_scale(layer_out, norm_gain)
    logits = jnp.dot(normed, head_weight, preferred_element_type=jnp.float32)
    row_peak = lax.optimization_barrier(jnp.max(logits, axis=1))
    log_total = row_peak + jnp.log(lax.optimization_barrier(jnp.sum(jnp.exp(logits - row_peak[:, None]), axis=1)))
    target_logit = jnp.take_along_axis(logits, targets[:, None].astype(jnp.int32), axis=1)[:, 0]
    token_logprob = target_logit - log_total
    token_loss = clipped_loss(token_logprob, rollout_logprob, advantages)
    return (layer_out, token_logprob, token_loss)
```

```python
import functools

import jax
import jax.numpy as jnp
from jax import lax
from jax.experimental import pallas as pl
from jax.experimental.pallas import tpu as pltpu
from jax.sharding import PartitionSpec as P

norm_epsilon = 1e-06
clip_low = 0.8
clip_high = 1.2
dual_bound = 3.0
MESH = pl.DeviceIdType.MESH


def clipped_loss(logprob, rollout_logprob, advantages):
    ratio = jnp.exp(logprob - rollout_logprob)
    surrogate = jnp.minimum(ratio * advantages, jnp.clip(ratio, clip_low, clip_high) * advantages)
    bounded = jnp.where(
        advantages < 0.0, jnp.maximum(surrogate, dual_bound * advantages), surrogate
    )
    return -bounded


def own_position(vocab_count):
    return lax.axis_index("dp") * vocab_count + lax.axis_index("vocab")


def exchange_kernel(count, vocab_count, kinds, *refs):
    number = len(kinds)
    ins, outs = refs[:number], refs[number : 2 * number]
    send_sem, recv_sem, local_sem = refs[2 * number :]
    me = own_position(vocab_count)
    barrier = pltpu.get_barrier_semaphore()

    def place(index):
        return (index // vocab_count, index % vocab_count)

    def source(which, target):
        if kinds[which] == "all":
            return ins[which]
        if kinds[which] == "group":
            return ins[which].at[target // vocab_count]
        return ins[which].at[target]

    def greet(step, carry):
        pl.semaphore_signal(
            barrier, inc=1, device_id=place((me + step) % count), device_id_type=MESH
        )
        return carry

    lax.fori_loop(1, count, greet, 0)
    pl.semaphore_wait(barrier, count - 1)

    def copy(which, target, sender):
        return pltpu.make_async_remote_copy(
            src_ref=source(which, target),
            dst_ref=outs[which].at[sender],
            send_sem=send_sem.at[which, target],
            recv_sem=recv_sem.at[which, sender],
            device_id=place(target),
            device_id_type=MESH,
        )

    def send(step, carry):
        target = (me + step) % count
        for which in range(number):
            copy(which, target, me).start()
        return carry

    lax.fori_loop(1, count, send, 0)
    for which in range(number):
        pltpu.make_async_copy(source(which, me), outs[which].at[me], local_sem.at[which]).start()

    def finish(step, carry):
        target = (me + step) % count
        sender = (me + count - step) % count
        for which in range(number):
            copy(which, target, me).wait_send()
            copy(which, target, sender).wait_recv()
        return carry

    lax.fori_loop(1, count, finish, 0)
    for which in range(number):
        pltpu.make_async_copy(source(which, me), outs[which].at[me], local_sem.at[which]).wait()


def exchange(arrays, kinds, count, vocab_count, identity):
    shapes = []
    for array, kind in zip(arrays, kinds):
        tail = array.shape if kind == "all" else array.shape[1:]
        shapes.append(jax.ShapeDtypeStruct((count,) + tail, array.dtype))
    number = len(arrays)
    return pl.pallas_call(
        functools.partial(exchange_kernel, count, vocab_count, kinds),
        out_shape=shapes,
        in_specs=[pl.BlockSpec(memory_space=pltpu.VMEM)] * number,
        out_specs=[pl.BlockSpec(memory_space=pltpu.VMEM)] * number,
        scratch_shapes=[
            pltpu.SemaphoreType.DMA((number, count)),
            pltpu.SemaphoreType.DMA((number, count)),
            pltpu.SemaphoreType.DMA((number,)),
        ],
        compiler_params=pltpu.CompilerParams(
            collective_id=identity, has_side_effects=True, vmem_limit_bytes=16 * 2**20
        ),
    )(*arrays)


def combine_kernel(
    bit_count,
    vocab_count,
    orders,
    cuts,
    part_ref,
    token_ref,
    gain_ref,
    layer,
    normed,
    held,
    *rest,
):
    slots = rest[:bit_count]
    send_sem, recv_sem, load_sem = rest[bit_count:]
    chains = len(orders)
    me = own_position(vocab_count)
    bits = [(me // (1 << b)) % 2 for b in range(bit_count)]

    def partner(b):
        other = me + (1 - 2 * bits[b]) * (1 << b)
        return (other // vocab_count, other % vocab_count)

    barrier = pltpu.get_barrier_semaphore()
    friends = [partner(b) for b in range(bit_count)]
    for friend in friends:
        pl.semaphore_signal(barrier, inc=1, device_id=friend, device_id_type=MESH)
    pl.semaphore_wait(barrier, len(friends))

    def index(chosen, low):
        return tuple(
            chosen[b] if b in chosen else slice(None) for b in range(bit_count - 1, low - 1, -1)
        )

    def span(chain):
        return pl.ds(cuts[chain], cuts[chain + 1] - cuts[chain])

    def load(chain):
        where = index({0: bits[0]}, 0) + (slice(None), span(chain))
        return pltpu.make_async_copy(
            part_ref.at[where],
            held.at[index({}, 1) + (slice(None), span(chain))],
            load_sem.at[chain],
        )

    def scatter(chain, stage):
        b = orders[chain][stage]
        if stage == 0:
            src = part_ref.at[index({0: 1 - bits[0]}, 0) + (slice(None), span(chain))]
        else:
            chosen = {f: bits[f] for f in orders[chain][1:stage]}
            chosen[b] = 1 - bits[b]
            src = held.at[index(chosen, 1) + (slice(None), span(chain))]
        free = bit_count - 1 - stage
        dst = slots[stage].at[(slice(None),) * (free + 1) + (span(chain),)]
        return pltpu.make_async_remote_copy(
            src_ref=src,
            dst_ref=dst,
            send_sem=send_sem.at[chain, stage],
            recv_sem=recv_sem.at[chain, stage],
            device_id=partner(b),
            device_id_type=MESH,
        )

    def add(chain, stage):
        order = orders[chain]
        fixed = order[1 : stage + 1]
        free = [f for f in range(bit_count - 1, 0, -1) if f not in fixed]
        blocks = 1 << len(free)

        def body(j, carry):
            values = {f: (j // (1 << q)) % 2 for q, f in enumerate(reversed(free))}
            at_slot = tuple(values[f] for f in free) + (slice(None), span(chain))
            values.update({f: bits[f] for f in fixed})
            at_held = index(values, 1) + (slice(None), span(chain))
            held[at_held] = (
                held[at_held].astype(jnp.float32) + slots[stage][at_slot].astype(jnp.float32)
            ).astype(jnp.bfloat16)
            return carry

        if stage < bit_count - 1:
            lax.fori_loop(0, blocks, body, 0)
        else:
            at_held = index({f: bits[f] for f in fixed}, 1) + (slice(None), span(chain))
            total = held[at_held].astype(jnp.float32)
            total = total + slots[stage][slice(None), span(chain)].astype(jnp.float32)
            total = total + token_ref[:, span(chain)].astype(jnp.float32)
            layer[:, span(chain)] = total.astype(jnp.bfloat16)

    for chain in range(chains):
        scatter(chain, 0).start()
    for chain in range(chains):
        load(chain).start()
    for stage in range(bit_count):
        for chain in range(chains):
            if stage == 0:
                load(chain).wait()
            scatter(chain, stage).wait_recv()
            add(chain, stage)
            if stage + 1 < bit_count:
                scatter(chain, stage + 1).start()

    rows = layer[...].astype(jnp.float32)
    mean_square = jnp.mean(rows * rows, axis=-1, keepdims=True)
    normed[...] = (rows * lax.rsqrt(mean_square + norm_epsilon) * gain_ref[...]).astype(
        jnp.bfloat16
    )
    for chain in range(chains):
        for stage in range(bit_count):
            scatter(chain, stage).wait_send()


def head_kernel(
    bit_count,
    vocab_count,
    orders,
    cuts,
    tile,
    normed_ref,
    layer_ref,
    label_ref,
    head_ref,
    stats_ref,
    group_ref,
    rows_all,
    logits,
    weights,
    ici_send,
    ici_recv,
    core_send,
    core_recv,
    weight_sem,
    own_sem,
    group_send,
    group_recv,
):
    chains = len(orders)
    me = own_position(vocab_count)
    my_vocab = lax.axis_index("vocab")
    bits = [(me // (1 << b)) % 2 for b in range(bit_count)]
    vocab_bits = vocab_count.bit_length() - 1
    columns = head_ref.shape[1]
    tiles = columns // tile
    stages = bit_count - 1
    widths = [cuts[c + 1] - cuts[c] for c in range(chains)]

    def partner(b):
        other = me + (1 - 2 * bits[b]) * (1 << b)
        return (other // vocab_count, other % vocab_count)

    def index(chosen):
        return tuple(
            chosen[b] if b in chosen else slice(None) for b in range(bit_count - 1, -1, -1)
        )

    def span(chain):
        return pl.ds(cuts[chain], widths[chain])

    turns = [(chain, 0) for chain in range(chains)] + [(chain, 1) for chain in range(chains)]

    def fetch(turn, column, slot):
        chain = turns[turn][0]
        return pltpu.make_async_copy(
            head_ref.at[span(chain), pl.ds(pl.multiple_of(column * tile, tile), tile)],
            weights.at[slot, pl.ds(0, widths[chain])],
            weight_sem.at[slot],
        )

    fetch(0, 0, 0).start()
    fetch(0, 1, 1).start()

    barrier = pltpu.get_barrier_semaphore()
    for b in range(bit_count):
        pl.semaphore_signal(barrier, inc=1, device_id=partner(b), device_id_type=MESH)
    pl.semaphore_wait(barrier, bit_count)

    own = pltpu.make_async_copy(
        normed_ref, rows_all.at[index({b: bits[b] for b in range(bit_count)})], own_sem.at[0]
    )
    own.start()
    own_group = pltpu.make_async_copy(layer_ref, group_ref.at[my_vocab], own_sem.at[1])
    own_group.start()
    own.wait()

    def remote(where, sends, recvs, b):
        return pltpu.make_async_remote_copy(
            src_ref=rows_all.at[where],
            dst_ref=rows_all.at[where],
            send_sem=sends,
            recv_sem=recvs,
            device_id=partner(b),
            device_id_type=MESH,
        )

    def spread(chain, stage):
        order = orders[chain]
        where = index({f: bits[f] for f in order[: bit_count - stage]}) + (slice(None), span(chain))
        return remote(
            where,
            ici_send.at[chain, stage],
            ici_recv.at[chain, stage],
            order[bit_count - 1 - stage],
        )

    def side(chain, half):
        bit = bits[orders[chain][1]]
        return bit if half == 0 else 1 - bit

    def across(chain, half):
        where = index({0: bits[0], orders[chain][1]: side(chain, half)}) + (
            slice(None),
            span(chain),
        )
        return remote(where, core_send.at[chain, half], core_recv.at[chain, half], 0)

    def group(b):
        held_count = vocab_count >> (b + 1)
        step = 1 << (b + 1)
        copies = []
        for q in range(held_count):
            position = q * step + my_vocab % step
            copies.append(
                pltpu.make_async_remote_copy(
                    src_ref=group_ref.at[position],
                    dst_ref=group_ref.at[position],
                    send_sem=group_send.at[b, q],
                    recv_sem=group_recv.at[b, q],
                    device_id=partner(b),
                    device_id_type=MESH,
                )
            )
        return copies

    for chain in range(chains):
        spread(chain, 0).start()

    def clear(j, carry):
        at = tuple((j // (1 << b)) % 2 for b in range(bit_count - 1, -1, -1))
        logits[at] = jnp.zeros(logits.shape[bit_count:], jnp.float32)
        return carry

    lax.fori_loop(0, 1 << bit_count, clear, 0)
    for stage in range(stages - 1):
        for chain in range(chains):
            spread(chain, stage).wait_recv()
            spread(chain, stage + 1).start()
            if stage == stages - 2:
                across(chain, 0).start()
    own_group.wait()

    count = len(turns)
    for turn in range(count):
        chain, half = turns[turn]
        if half == 0:
            across(chain, 0).wait_recv()
        else:
            if chain == 0:
                for other in range(chains):
                    spread(other, stages - 1).wait_recv()
                    across(other, 1).start()
                for copy in group(vocab_bits - 1):
                    copy.start()
            across(chain, 1).wait_recv()
            if chain > 0:
                b = vocab_bits - 1 - chain
                if b >= 0:
                    for copy in group(b + 1):
                        copy.wait_recv()
                    for copy in group(b):
                        copy.start()
        fixed = orders[chain][1]
        where = index({fixed: side(chain, half)})

        def body(column, carry):
            slot = (turn * tiles + column) % 3
            fetch(turn, column, slot).wait()

            @pl.when(column + 2 < tiles)
            def _():
                fetch(turn, column + 2, (turn * tiles + column + 2) % 3).start()

            if turn + 1 < count:

                @pl.when(column + 2 >= tiles)
                def _():
                    fetch(
                        turn + 1, column + 2 - tiles, (turn * tiles + column + 2) % 3
                    ).start()

            left = rows_all[where + (slice(None), span(chain))]
            shape = left.shape[:-1]
            left = left.reshape(-1, widths[chain])
            product = jnp.dot(
                left, weights[slot, : widths[chain]], preferred_element_type=jnp.float32
            ).reshape(shape + (tile,))
            at = where + (slice(None), pl.ds(pl.multiple_of(column * tile, tile), tile))
            logits[at] += product
            return carry

        lax.fori_loop(0, tiles, body, 0)

    waited = vocab_bits - 1 - (chains - 1)
    for b in range(max(waited, 0), -1, -1):
        for copy in group(b):
            if b < waited:
                copy.start()
            copy.wait_recv()

    first_column = me * columns
    lanes = lax.broadcasted_iota(jnp.int32, (1, columns), 1) + first_column
    stat_lane = lax.broadcasted_iota(jnp.int32, (1, 128), 1)

    def reduce_block(j, carry):
        at = tuple((j // (1 << b)) % 2 for b in range(bit_count - 1, -1, -1))
        values = logits[at]
        peak = jnp.max(values, axis=1, keepdims=True)
        total = jnp.sum(jnp.exp(values - peak), axis=1, keepdims=True)
        match = lanes == label_ref[j]
        picked = jnp.sum(jnp.where(match, values, 0.0), axis=1, keepdims=True)
        stats_ref[j] = jnp.where(
            stat_lane == 0, peak, jnp.where(stat_lane == 1, total, picked)
        )
        return carry

    lax.fori_loop(0, 1 << bit_count, reduce_block, 0)

    for chain in range(chains):
        for stage in range(stages):
            spread(chain, stage).wait_send()
        across(chain, 0).wait_send()
        across(chain, 1).wait_send()
    for b in range(vocab_bits):
        for copy in group(b):
            copy.wait_send()


def axis_plan(device_count, vocab_count, width):
    bit_count = device_count.bit_length() - 1
    vocab_bits = vocab_count.bit_length() - 1
    low = vocab_bits + (bit_count - vocab_bits) // 2
    first = list(range(1, vocab_bits))
    second = list(range(vocab_bits, low))
    third = list(range(low, bit_count))
    orders = [[0] + first + second + third, [0] + second + first + third, [0] + third + first + second]
    lanes = width // 128
    cuts = [0, 128 * (lanes // 3), 128 * (2 * lanes // 3), width]
    return bit_count, orders, cuts


def combine(part, tokens, gain, device_count, vocab_count):
    rows, width = tokens.shape
    bit_count, orders, cuts = axis_plan(device_count, vocab_count, width)
    part = part.reshape((2,) * bit_count + (rows, width))
    scratch = [pltpu.VMEM((2,) * (bit_count - 1) + (rows, width), jnp.bfloat16)]
    for stage in range(bit_count):
        scratch.append(pltpu.VMEM((2,) * (bit_count - 1 - stage) + (rows, width), jnp.bfloat16))
    chains = len(orders)
    scratch += [pltpu.SemaphoreType.DMA((chains, bit_count))] * 2
    scratch += [pltpu.SemaphoreType.DMA((chains,))]
    return pl.pallas_call(
        functools.partial(combine_kernel, bit_count, vocab_count, orders, cuts),
        out_shape=[jax.ShapeDtypeStruct((rows, width), jnp.bfloat16)] * 2,
        in_specs=[
            pl.BlockSpec(memory_space=pl.ANY),
            pl.BlockSpec(memory_space=pltpu.VMEM),
            pl.BlockSpec(memory_space=pltpu.VMEM),
        ],
        out_specs=[pl.BlockSpec(memory_space=pltpu.VMEM)] * 2,
        scratch_shapes=scratch,
        compiler_params=pltpu.CompilerParams(
            collective_id=1, has_side_effects=True, vmem_limit_bytes=58 * 2**20
        ),
    )(part, tokens, gain)


def head(normed, layer, labels, head_weight, device_count, vocab_count):
    rows, width = normed.shape
    columns = head_weight.shape[1]
    tile = 512 if columns % 512 == 0 else 128
    bit_count, orders, cuts = axis_plan(device_count, vocab_count, width)
    chains = len(orders)
    vocab_bits = vocab_count.bit_length() - 1
    widest = max(cuts[c + 1] - cuts[c] for c in range(chains))
    lead = (2,) * bit_count
    stats, group = pl.pallas_call(
        functools.partial(head_kernel, bit_count, vocab_count, orders, cuts, tile),
        out_shape=[
            jax.ShapeDtypeStruct((device_count, rows, 128), jnp.float32),
            jax.ShapeDtypeStruct((vocab_count, rows, width), jnp.bfloat16),
        ],
        in_specs=[
            pl.BlockSpec(memory_space=pltpu.VMEM),
            pl.BlockSpec(memory_space=pltpu.VMEM),
            pl.BlockSpec(memory_space=pltpu.VMEM),
            pl.BlockSpec(memory_space=pl.ANY),
        ],
        out_specs=[
            pl.BlockSpec(memory_space=pltpu.VMEM),
            pl.BlockSpec(memory_space=pl.ANY),
        ],
        scratch_shapes=[
            pltpu.VMEM(lead + (rows, width), jnp.bfloat16),
            pltpu.VMEM(lead + (rows, columns), jnp.float32),
            pltpu.VMEM((3, widest, tile), jnp.bfloat16),
            pltpu.SemaphoreType.DMA((chains, bit_count - 1)),
            pltpu.SemaphoreType.DMA((chains, bit_count - 1)),
            pltpu.SemaphoreType.DMA((chains, 2)),
            pltpu.SemaphoreType.DMA((chains, 2)),
            pltpu.SemaphoreType.DMA((3,)),
            pltpu.SemaphoreType.DMA((2,)),
            pltpu.SemaphoreType.DMA((vocab_bits, vocab_count // 2)),
            pltpu.SemaphoreType.DMA((vocab_bits, vocab_count // 2)),
        ],
        compiler_params=pltpu.CompilerParams(
            collective_id=3, has_side_effects=True, vmem_limit_bytes=60 * 2**20
        ),
    )(normed, layer, labels, head_weight)
    return stats, group.reshape(vocab_count * rows, width)


def per_device(
    tokens,
    expert_hidden,
    routes,
    route_weight,
    expert_weight,
    norm_gain,
    head_weight,
    targets,
    rollout_logprob,
    advantages,
):
    vocab_count = lax.axis_size("vocab")
    device_count = lax.axis_size(("dp", "vocab"))
    experts = device_count // 2
    group_count = tokens.shape[0]
    sub_rows = group_count // vocab_count
    top_count = routes.shape[1]
    sub_start = lax.axis_index("vocab") * sub_rows
    mine_tokens = lax.dynamic_slice_in_dim(tokens, sub_start, sub_rows, 0)
    mine_hidden = lax.dynamic_slice_in_dim(expert_hidden, sub_start, sub_rows, 0)
    mine_routes = lax.dynamic_slice_in_dim(routes, sub_start, sub_rows, 0)
    mine_weights = lax.dynamic_slice_in_dim(route_weight, sub_start, sub_rows, 0)
    labels_sub = lax.dynamic_slice_in_dim(targets, sub_start, sub_rows, 0)
    hidden_rows = mine_hidden.reshape(-1, mine_hidden.shape[2])
    half_width = hidden_rows.shape[1] // 2
    route_list = mine_routes.reshape(-1)
    weight_list = mine_weights.reshape(-1)
    named = jnp.where(
        lax.iota(jnp.int32, experts)[:, None] == route_list[None, :], weight_list[None, :], 0.0
    )
    row_of = lax.iota(jnp.int32, sub_rows * top_count) // top_count
    same_row = lax.iota(jnp.int32, sub_rows)[:, None] == row_of[None, :]
    select = jnp.where(same_row[None], named[:, None], 0.0).astype(jnp.bfloat16)
    select = select.reshape(experts * sub_rows, sub_rows * top_count)
    dense = jnp.dot(select, hidden_rows, preferred_element_type=jnp.float32).astype(jnp.bfloat16)
    dense = dense.reshape(experts, sub_rows, 2, half_width).transpose(0, 2, 1, 3)
    dense = dense.reshape(device_count, sub_rows, half_width)
    label_tile = jnp.broadcast_to(
        jnp.pad(labels_sub, (0, 128 - sub_rows))[None, :], (8, 128)
    )
    received, label_tiles = exchange(
        [dense, label_tile], ("each", "all"), device_count, vocab_count, 0
    )
    labels = label_tiles[:, 0, :sub_rows].reshape(-1)
    part = jnp.dot(
        received.reshape(device_count * sub_rows, half_width),
        expert_weight[0],
        preferred_element_type=jnp.float32,
    ).astype(jnp.bfloat16)
    layer_sub, normed = combine(
        part, mine_tokens, norm_gain[None, :], device_count, vocab_count
    )
    labels = labels.reshape(device_count, sub_rows, 1)
    stats_rows, group_layer = head(
        normed, layer_sub, labels, head_weight, device_count, vocab_count
    )
    stats = stats_rows[:, :, :8].reshape(-1, group_count, 8).transpose(0, 2, 1)
    (stats_all,) = exchange([stats], ("group",), device_count, vocab_count, 2)
    peaks, totals, picks = stats_all[:, 0], stats_all[:, 1], stats_all[:, 2]
    peak = jnp.max(peaks, axis=0)
    total = jnp.sum(totals * jnp.exp(peaks - peak[None]), axis=0)
    token_logprob = jnp.sum(picks, axis=0) - (peak + jnp.log(total))
    token_loss = clipped_loss(token_logprob, rollout_logprob, advantages)
    return (group_layer, token_logprob, token_loss)


def solution(mesh):
    placed = (
        P("dp", None),
        P("dp", None, None),
        P("dp", None),
        P("dp", None),
        P(("dp", "vocab"), None, None),
        P(),
        P(None, ("dp", "vocab")),
        P("dp"),
        P("dp"),
        P("dp"),
    )
    return jax.shard_map(
        per_device,
        mesh=mesh,
        in_specs=placed,
        out_specs=(P("dp", None), P("dp"), P("dp")),
        check_vma=False,
    )
```
